32 devices in a mesh: groups: 2 (over x), space: 16 (over z, y, core).
Axes of the slice: x: 2, y: 2, z: 4, core: 2. Of those that a mesh axis runs over, the one named last changes fastest.
Arguments:
- field: bfloat16 [64, 256, 1024], P(('groups', 'space')), parts along dimension 0, may hold values from -3 to 3
- history: bfloat16 [3, 64, 1024], P(None, ('groups', 'space')), parts along dimension 1, may hold values from -3 to 3
- source: bfloat16 [64, 256, 1024], P(('groups', 'space')), parts along dimension 0, may hold values from -6 to 6
- row_conduct: float32 [2048], P('groups'), parts along dimension 0, may hold values from 0.25 to 2
- col_conduct: float32 [64, 1024], P(('groups', 'space')), parts along dimension 0, may hold values from 0.25 to 2
Outputs:
- spectrum: bfloat16 [64, 256, 1024], P('groups', 'space'), parts along dimension 0
The draws below stay inside these ranges and needn't reach their ends.
There are 2 independent parts, one for each index of `groups`. The reference program is written for one: setup_inputs(seed, part) draws one part's arguments, and reference() takes and returns one part's arrays. A program takes and returns all parts, laid end to end along the dimension named above; each array names one. Nothing has to cross between parts.
All inputs are finite; a program needn't handle non-finite values.
Results may differ from the reference program's by a relative error of at most 0.0045.
Values may be sent and summed in bfloat16 or wider, within the bound.
No kernel may reach another device: no remote copies, remote signals or barrier semaphores. Data moves between devices by JAX's collectives and lax.ppermute only.
A program may use at most 64 MiB of HBM per device.

```python
import math
import jax
import jax.numpy as jnp

NC = 1024
STEPS = 256
SWEEPS = 4
NR = 32


def level_of(stream_key, shape, pieces, least, largest):
    gain = 1.0
    for position, parts in pieces:
        draws = jax.random.uniform(jax.random.fold_in(jax.random.fold_in(stream_key, 6), position), (parts,), jnp.float32, least / len(pieces), largest / len(pieces))
        gain = gain * jnp.repeat(jnp.exp(draws), shape[position] // parts).reshape((-1,) + (1,) * (len(shape) - 1 - position))
    return gain


def centred(key, extent, scale, limit, pieces=(), kind=jnp.bfloat16):
    level = level_of(key, extent, pieces, -0.22, 0.18) if pieces else 1.0
    drawn = jax.random.normal(key, extent, jnp.float32) * scale * level
    return jnp.minimum(jnp.maximum(drawn, -limit), limit).astype(kind)


def setup_inputs(seed: int = 0, part: int = 0) -> dict:
    key_list = jax.random.split(jax.random.key(seed), 6)
    part_splits = jax.random.split(jax.random.fold_in(key_list[5], part), 6)
    return {
        "field": centred(part_splits[0], (NR, STEPS, NC), 0.5, 3.0, ((0, 16),)),
        "history": centred(part_splits[1], (3, NR, NC), 0.5, 3.0, ((1, 16),)),
        "source": centred(part_splits[2], (NR, STEPS, NC), 1.0, 6.0, ((0, 16),)),
        "row_conduct": jnp.clip(jnp.exp(jax.random.uniform(part_splits[3], (NC,), jnp.float32, math.log(0.25), math.log(2.0))), 0.25, 2.0),
        "col_conduct": jnp.clip(jnp.exp(math.log(2.0) - 2.0794415 * jax.random.uniform(part_splits[4], (NR, NC), jnp.float32) ** level_of(part_splits[4], (NR, NC), ((0, 16),), -0.2, 0.2)), 0.25, 2.0),
    }


def lam_tables(first_pair, pair_count, step_count):
    pair = first_pair + jnp.arange(pair_count, dtype=jnp.int32)
    half = step_count // 2

    def symbol(freq):
        theta = 2.0 * math.pi / step_count * (freq % step_count).astype(jnp.float32)
        real_part = 11.0 / 6.0 - 3.0 * jnp.cos(theta) + 1.5 * jnp.cos(2.0 * theta) - jnp.cos(3.0 * theta) / 3.0
        imag_part = 3.0 * jnp.sin(theta) - 1.5 * jnp.sin(2.0 * theta) + jnp.sin(3.0 * theta) / 3.0
        return (real_part, imag_part)
    first_re, cross = symbol(pair)
    second_re, unused = symbol(jnp.where(pair == 0, half, pair))
    return (first_re, second_re, cross)

def relax(current, upper, lower, rhs, tables, row_c, col_c, left_c):
    first_re, second_re, cross = tables
    diag = 0.5 * (2.0 * row_c[None, :] + col_c + left_c)
    if current is None:
        total = rhs
    else:
        beside = row_c[None, None, :] * (upper + lower) + col_c[:, None, :] * jnp.roll(current, -1, axis=2) + left_c[:, None, :] * jnp.roll(current, 1, axis=2)
        total = rhs + 0.5 * beside
    rows, slots, cols = total.shape
    split = total.reshape(rows, slots // 2, 2, cols)
    right_a = split[:, :, 0]
    right_b = split[:, :, 1]
    p_first = first_re[None, :, None] + diag[:, None, :]
    p_second = second_re[None, :, None] + diag[:, None, :]
    skew = cross[None, :, None]
    det = p_first * p_second + skew * skew
    first = (p_second * right_a + skew * right_b) / det
    second = (p_first * right_b - skew * right_a) / det
    return jnp.stack([first, second], axis=2).reshape(rows, slots, cols)

def reference(field, history, source, row_conduct, col_conduct):
    values = field.astype(jnp.float32)
    earlier = jnp.transpose(history, (1, 0, 2)).astype(jnp.float32)
    extended = jnp.concatenate([earlier, values], axis=1)
    backward = 11.0 / 6.0 * extended[:, 3:] - 3.0 * extended[:, 2:-1] + 1.5 * extended[:, 1:-2] - extended[:, :-3] / 3.0
    row_flux = row_conduct[None, None, :] * (2.0 * values - jnp.roll(values, 1, axis=0) - jnp.roll(values, -1, axis=0))
    left_face = jnp.roll(col_conduct, 1, axis=1)
    column_flux = col_conduct[:, None, :] * (values - jnp.roll(values, -1, axis=2)) + left_face[:, None, :] * (values - jnp.roll(values, 1, axis=2))
    residual = source.astype(jnp.float32) - backward - 0.5 * (row_flux + column_flux)
    fourier = jnp.fft.rfft(residual, axis=1)
    half = STEPS // 2
    real_part = jnp.real(fourier).astype(jnp.float32)
    imag_part = jnp.imag(fourier).astype(jnp.float32)
    imag_low = imag_part[:, :half].at[:, 0].set(real_part[:, half])
    packed = jnp.stack([real_part[:, :half], imag_low], axis=2).reshape(NR, STEPS, NC) / math.sqrt(STEPS)
    tables = lam_tables(0, half, STEPS)
    current = relax(None, None, None, packed, tables, row_conduct, col_conduct, left_face)
    for sweep in range(SWEEPS - 1):
        current = relax(current, jnp.roll(current, 1, axis=0), jnp.roll(current, -1, axis=0), packed, tables, row_conduct, col_conduct, left_face)
    return current.astype(jnp.bfloat16)
```

```python
import functools
import math

import jax
import jax.numpy as jnp
import numpy as np
from jax import lax
from jax.experimental import pallas as pl
from jax.experimental.pallas import tpu as pltpu
from jax.sharding import PartitionSpec as P

SWEEPS = 4
VMEM = pl.BlockSpec(memory_space=pltpu.VMEM)
SMEM = pl.BlockSpec(memory_space=pltpu.SMEM)


def slot_order(steps, devices):
    share = steps // devices
    order = []
    for core in range(2):
        for chip in range(devices // 2):
            first = (chip * 2 + core) * share
            order += list(range(first, first + share, 2)) + list(range(first + 1, first + share, 2))
    return np.array(order)


def transform_tables(steps, devices):
    index = np.arange(steps)
    freqs = np.where(index == 1, steps // 2, index // 2)
    use_cos = (index % 2 == 0) | (index == 1)
    phase = 2.0 * np.pi / steps * (freqs[:, None] * index[None, :] % steps)
    table = np.where(use_cos[:, None], np.cos(phase), -np.sin(phase)) / math.sqrt(steps)
    table = table[slot_order(steps, devices)]
    high = table.astype(jnp.bfloat16)
    low = (table - high.astype(np.float64)).astype(jnp.bfloat16)
    return high, low


def symbol_tables(steps):
    pair = np.arange(steps // 2)

    def real_part(freq):
        theta = 2.0 * np.pi / steps * freq
        return 11.0 / 6.0 - 3.0 * np.cos(theta) + 1.5 * np.cos(2.0 * theta) - np.cos(3.0 * theta) / 3.0

    theta = 2.0 * np.pi / steps * pair
    cross = 3.0 * np.sin(theta) - 1.5 * np.sin(2.0 * theta) + np.sin(3.0 * theta) / 3.0
    second = np.where(pair == 0, steps // 2, pair)
    return np.stack([real_part(pair), real_part(second), cross]).astype(np.float32)


def transform_kernel(
    outer, scal, field, halo, hist, source, row_c, col_c, high, low, own, other, r_high, r_low
):
    core, chip = scal[0], scal[1]
    row = core if outer else 1 - core
    beside = 1 - row
    steps, cols = r_high.shape
    rc = 0.5 * row_c[...]
    cc = 0.5 * col_c[pl.ds(row, 1)]
    cl = pltpu.roll(cc, 1, 1)
    diag = 2.0 * rc + cc + cl
    tile = 16

    def at(i, before):
        rows = pl.ds(pl.multiple_of(i * tile, tile), tile)
        c = field[row, rows, :].astype(jnp.float32)
        near = field[beside, rows, :].astype(jnp.float32) + halo[0, rows, :].astype(jnp.float32)
        seq = jnp.concatenate([before, c], axis=0)
        back = (
            11.0 / 6.0 * c
            - 3.0 * seq[7 : 7 + tile]
            + 1.5 * seq[6 : 6 + tile]
            - seq[5 : 5 + tile] / 3.0
        )
        flux = diag * c - rc * near - cc * pltpu.roll(c, cols - 1, 1) - cl * pltpu.roll(c, 1, 1)
        res = source[row, rows, :].astype(jnp.float32) - back - flux
        upper = res.astype(jnp.bfloat16)
        r_high[rows, :] = upper
        r_low[rows, :] = (res - upper.astype(jnp.float32)).astype(jnp.bfloat16)
        return c[tile - 8 :]

    lax.fori_loop(0, steps // tile, at, hist[row])
    half = steps // 2
    chips, share, _ = own.shape
    width = min(cols, 256)
    for ref, which in ((other, 1 - core), (own, core)):
        part = pl.ds(pl.multiple_of(which * half, half), half)
        for j in range(0, cols, width):
            a, b = r_high[:, j : j + width], r_low[:, j : j + width]
            acc = jnp.dot(high[part, :], a, preferred_element_type=jnp.float32)
            acc += jnp.dot(high[part, :], b, preferred_element_type=jnp.float32)
            acc += jnp.dot(low[part, :], a, preferred_element_type=jnp.float32)
            acc = acc.astype(jnp.bfloat16)
            for g in range(chips):
                ref[g ^ chip, :, j : j + width] = acc[g * share : (g + 1) * share]


def transform(outer, scal, field, halo, hist, source, row_c, col_c, tables, devices):
    _, steps, cols = field.shape
    shape = jax.ShapeDtypeStruct((devices // 2, steps // devices, cols), jnp.bfloat16)
    return pl.pallas_call(
        functools.partial(transform_kernel, outer),
        out_shape=(shape, shape),
        in_specs=[SMEM] + [VMEM] * 8,
        out_specs=(VMEM, VMEM),
        scratch_shapes=[pltpu.VMEM((steps, cols), jnp.bfloat16)] * 2,
        cost_estimate=pl.CostEstimate(
            flops=6 * steps * steps * cols, bytes_accessed=4 * steps * cols * 2, transcendentals=0
        ),
        name="transform",
    )(scal, field, halo, hist, source, row_c, col_c, *tables)


def assemble_kernel(own, other, *outs):
    for k, out in enumerate(outs):
        out[0] = own[k + 1]
        out[1] = other[k + 1]


def assemble(own, other):
    chips, share, cols = own.shape
    return pl.pallas_call(
        assemble_kernel,
        out_shape=[jax.ShapeDtypeStruct((2, share, cols), own.dtype)] * (chips - 1),
        in_specs=[VMEM] * 2,
        out_specs=[VMEM] * (chips - 1),
        cost_estimate=pl.CostEstimate(
            flops=0, bytes_accessed=4 * chips * share * cols * 2, transcendentals=0
        ),
        name="assemble",
    )(own, other)


def coefficient_kernel(scal, row_c, symbols, *refs):
    *faces, first, second, cross, ahead, behind = refs
    core, chip = scal[0], scal[1]
    rc = 0.5 * row_c[...]
    one, two, skew = symbols[0], symbols[1], symbols[2]
    for k, face in enumerate(faces):
        for j in range(4):
            side = core if j < 2 else 1 - core
            at = (chip ^ k) * 4 + side * 2 + j % 2
            cc = 0.5 * face[j : j + 1, :]
            cl = pltpu.roll(cc, 1, 1)
            diag = 2.0 * rc + cc + cl
            p0 = one + diag
            p1 = two + diag
            inverse = 1.0 / (p0 * p1 + skew * skew)
            first[at] = p1 * inverse
            second[at] = p0 * inverse
            cross[at] = skew * inverse
            ahead[at] = cc
            behind[at] = cl


def coefficients(scal, row_c, symbols, faces):
    rows = 4 * len(faces)
    pairs = symbols.shape[1]
    cols = row_c.shape[1]
    big = jax.ShapeDtypeStruct((rows, pairs, cols), jnp.float32)
    thin = jax.ShapeDtypeStruct((rows, 1, cols), jnp.float32)
    return pl.pallas_call(
        coefficient_kernel,
        out_shape=[big, big, big, thin, thin],
        in_specs=[SMEM] + [VMEM] * (2 + len(faces)),
        out_specs=[VMEM] * 5,
        cost_estimate=pl.CostEstimate(
            flops=10 * rows * pairs * cols, bytes_accessed=12 * rows * pairs * cols, transcendentals=0
        ),
        name="coefficients",
    )(scal, row_c, symbols, *faces)


def sweep_kernel(scal, row_c, first, second, cross, ahead, behind, *refs):
    *blocks, out, rhs_re, rhs_im, a_re, a_im, b_re, b_im, mixed = refs
    core, chip = scal[0], scal[1]
    rows, pairs, cols = rhs_re.shape
    chips = rows // 4
    rc = 0.5 * row_c[...]

    def solve(i, t0, t1):
        s = cross[i]
        return first[i] * t0 + s * t1, second[i] * t1 - s * t0

    def enter(block, k, side, outer):
        owner = core if side == 0 else 1 - core
        row = owner if outer else 1 - owner
        i = (chip ^ k) * 4 + owner * 2 + row
        both = block.astype(jnp.float32)
        t0, t1 = both[:pairs], both[pairs:]
        rhs_re[i], rhs_im[i] = t0, t1
        a_re[i], a_im[i] = solve(i, t0, t1)

    per = chips + 1
    for outer in (False, True):
        own, other, *far = blocks[per * outer : per * (outer + 1)]
        enter(own[0], 0, 0, outer)
        enter(other[0], 0, 1, outer)
        for k, block in enumerate(far):
            enter(block[0], k + 1, 0, outer)
            enter(block[1], k + 1, 1, outer)

    def neighbours(z, i, up, down):
        c = z[i]
        return (
            rc * (z[up] + z[down])
            + ahead[i] * pltpu.roll(c, cols - 1, 1)
            + behind[i] * pltpu.roll(c, 1, 1)
        )

    def sweep(src, dst):
        def at(i, carry):
            up = jnp.where(i == 0, rows - 1, i - 1)
            down = jnp.where(i == rows - 1, 0, i + 1)
            t0 = rhs_re[i] + neighbours(src[0], i, up, down)
            t1 = rhs_im[i] + neighbours(src[1], i, up, down)
            z0, z1 = solve(i, t0, t1)
            if dst is None:
                for j in range(mixed.shape[0]):
                    lanes = slice(j * 128, (j + 1) * 128)
                    mixed[j, pl.ds(0, pairs, stride=2), :] = z0[:, lanes]
                    mixed[j, pl.ds(1, pairs, stride=2), :] = z1[:, lanes]
                    out[i, :, lanes] = mixed[j].astype(out.dtype)
            else:
                dst[0][i], dst[1][i] = z0, z1
            return carry

        lax.fori_loop(0, rows, at, 0)

    src, dst = (a_re, a_im), (b_re, b_im)
    for step in range(SWEEPS - 1):
        sweep(src, None if step == SWEEPS - 2 else dst)
        src, dst = dst, src


def sweeps(scal, row_c, coeffs, blocks):
    rows, pairs, cols = coeffs[0].shape
    return pl.pallas_call(
        sweep_kernel,
        out_shape=jax.ShapeDtypeStruct((rows, 2 * pairs, cols), jnp.bfloat16),
        in_specs=[SMEM] + [VMEM] * (6 + len(blocks)),
        out_specs=VMEM,
        scratch_shapes=[pltpu.VMEM((rows, pairs, cols), jnp.float32)] * 6
        + [pltpu.VMEM((cols // 128, 2 * pairs, 128), jnp.float32)],
        cost_estimate=pl.CostEstimate(
            flops=80 * rows * pairs * cols, bytes_accessed=60 * rows * pairs * cols, transcendentals=0
        ),
        name="sweeps",
    )(scal, row_c, *coeffs, *blocks)


def on_device(field, history, source, row_conduct, col_conduct):
    devices = lax.axis_size("space")
    steps, cols = field.shape[1:]
    me = lax.axis_index("space")
    core, chip = me % 2, me // 2
    scal = jnp.stack([core, chip]).astype(jnp.int32)
    row_c = row_conduct.reshape(1, cols)
    partner = [(i, i ^ 1) for i in range(devices)]
    across = [(i, (i - 1 if i % 2 == 0 else i + 1) % devices) for i in range(devices)]

    def between(x, k):
        return lax.ppermute(x, "space", [(i, i ^ (2 * k)) for i in range(devices)])

    far_halo = lax.ppermute(lax.dynamic_slice_in_dim(field, core, 1, 0), "space", across)
    near_halo = lax.ppermute(lax.dynamic_slice_in_dim(field, 1 - core, 1, 0), "space", partner)
    face = jnp.concatenate([col_conduct, lax.ppermute(col_conduct, "space", partner)], axis=0)
    tables = transform_tables(steps, devices)
    earlier = jnp.pad(
        jnp.transpose(history, (1, 0, 2)).astype(jnp.float32), ((0, 0), (5, 0), (0, 0))
    )

    blocks = []
    faces = [face]
    for outer, halo in ((False, near_halo), (True, far_halo)):
        own, other = transform(
            outer, scal, field, halo, earlier, source, row_c, col_conduct, tables, devices
        )
        other = lax.ppermute(other, "space", partner)
        packs = assemble(own, other)
        blocks += [own, other] + [between(pack, k + 1) for k, pack in enumerate(packs)]
        if not outer:
            faces += [between(face, k) for k in range(1, devices // 2)]
    pairs = steps // devices // 2
    symbols = lax.dynamic_slice_in_dim(jnp.asarray(symbol_tables(steps)), me * pairs, pairs, 1)
    coeffs = coefficients(scal, row_c, symbols[:, :, None], faces)
    return sweeps(scal, row_c, coeffs, blocks)


def solution(mesh):
    in_specs = (
        P(("groups", "space"), None, None),
        P(None, ("groups", "space"), None),
        P(("groups", "space"), None, None),
        P("groups"),
        P(("groups", "space"), None),
    )
    out_specs = P("groups", "space", None)
    return jax.shard_map(
        on_device, mesh=mesh, in_specs=in_specs, out_specs=out_specs, check_vma=False
    )
```

```python
import functools
import math

import jax
import jax.numpy as jnp
import numpy as np
from jax import lax
from jax.experimental import pallas as pl
from jax.experimental.pallas import tpu as pltpu
from jax.sharding import PartitionSpec as P

SWEEPS = 4
VMEM = pl.BlockSpec(memory_space=pltpu.VMEM)
SMEM = pl.BlockSpec(memory_space=pltpu.SMEM)


def slot_order(steps, devices):
    share = steps // devices
    order = []
    for core in range(2):
        for chip in range(devices // 2):
            first = (chip * 2 + core) * share
            order += list(range(first, first + share, 2)) + list(range(first + 1, first + share, 2))
    return np.array(order)


def transform_tables(steps, devices):
    index = np.arange(steps)
    freqs = np.where(index == 1, steps // 2, index // 2)
    use_cos = (index % 2 == 0) | (index == 1)
    phase = 2.0 * np.pi / steps * (freqs[:, None] * index[None, :] % steps)
    table = np.where(use_cos[:, None], np.cos(phase), -np.sin(phase)) / math.sqrt(steps)
    table = table[slot_order(steps, devices)]
    high = table.astype(jnp.bfloat16)
    low = (table - high.astype(np.float64)).astype(jnp.bfloat16)
    return high, low


def symbol_tables(steps):
    pair = np.arange(steps // 2)

    def real_part(freq):
        theta = 2.0 * np.pi / steps * freq
        return 11.0 / 6.0 - 3.0 * np.cos(theta) + 1.5 * np.cos(2.0 * theta) - np.cos(3.0 * theta) / 3.0

    theta = 2.0 * np.pi / steps * pair
    cross = 3.0 * np.sin(theta) - 1.5 * np.sin(2.0 * theta) + np.sin(3.0 * theta) / 3.0
    second = np.where(pair == 0, steps // 2, pair)
    return np.stack([real_part(pair), real_part(second), cross]).astype(np.float32)


def transform_kernel(outer, scal, field, halo, hist, source, row_c, col_c, high, low, own, other, *refs):
    *spare, r_high, r_low = refs
    core, chip = scal[0], scal[1]
    row = core if outer else 1 - core
    beside = 1 - row
    steps, cols = r_high.shape
    rc = 0.5 * row_c[...]
    cc = 0.5 * col_c[pl.ds(row, 1)]
    cl = pltpu.roll(cc, 1, 1)
    diag = 2.0 * rc + cc + cl
    tile = 16
    if spare:
        spare[0][0] = field[beside]

    def at(i, before):
        rows = pl.ds(pl.multiple_of(i * tile, tile), tile)
        c = field[row, rows, :].astype(jnp.float32)
        near = field[beside, rows, :].astype(jnp.float32) + halo[0, rows, :].astype(jnp.float32)
        seq = jnp.concatenate([before, c], axis=0)
        back = (
            11.0 / 6.0 * c
            - 3.0 * seq[7 : 7 + tile]
            + 1.5 * seq[6 : 6 + tile]
            - seq[5 : 5 + tile] / 3.0
        )
        flux = diag * c - rc * near - cc * pltpu.roll(c, cols - 1, 1) - cl * pltpu.roll(c, 1, 1)
        res = source[row, rows, :].astype(jnp.float32) - back - flux
        upper = res.astype(jnp.bfloat16)
        r_high[rows, :] = upper
        r_low[rows, :] = (res - upper.astype(jnp.float32)).astype(jnp.bfloat16)
        return c[tile - 8 :]

    lax.fori_loop(0, steps // tile, at, hist[row])
    half = steps // 2
    chips, share, _ = own.shape
    width = min(cols, 256)
    for ref, which in ((other, 1 - core), (own, core)):
        part = pl.ds(pl.multiple_of(which * half, half), half)
        for j in range(0, cols, width):
            a, b = r_high[:, j : j + width], r_low[:, j : j + width]
            acc = jnp.dot(high[part, :], a, preferred_element_type=jnp.float32)
            acc += jnp.dot(high[part, :], b, preferred_element_type=jnp.float32)
            acc += jnp.dot(low[part, :], a, preferred_element_type=jnp.float32)
            acc = acc.astype(jnp.bfloat16)
            for g in range(chips):
                ref[g ^ chip, :, j : j + width] = acc[g * share : (g + 1) * share]


def transform(outer, scal, field, halo, hist, source, row_c, col_c, tables, devices):
    _, steps, cols = field.shape
    shape = jax.ShapeDtypeStruct((devices // 2, steps // devices, cols), jnp.bfloat16)
    spare = [] if outer else [jax.ShapeDtypeStruct((1, steps, cols), jnp.bfloat16)]
    return pl.pallas_call(
        functools.partial(transform_kernel, outer),
        out_shape=[shape, shape] + spare,
        in_specs=[SMEM] + [VMEM] * 8,
        out_specs=[VMEM] * (2 + len(spare)),
        scratch_shapes=[pltpu.VMEM((steps, cols), jnp.bfloat16)] * 2,
        cost_estimate=pl.CostEstimate(
            flops=6 * steps * steps * cols, bytes_accessed=4 * steps * cols * 2, transcendentals=0
        ),
        compiler_params=pltpu.CompilerParams(vmem_limit_bytes=8 * 2**20),
        name="transform",
    )(scal, field, halo, hist, source, row_c, col_c, *tables)


def put_face(face, out, first):
    high = face[...].astype(jnp.bfloat16)
    low = (face[...] - high.astype(jnp.float32)).astype(jnp.bfloat16)
    out[first : first + 8, :] = jnp.concatenate([high, low], axis=0)


def get_face(pack, first):
    both = pack[first : first + 8, :].astype(jnp.float32)
    return both[:4] + both[4:]


def assemble_kernel(phases, face, *refs):
    ins, outs = refs[: 2 * phases], refs[2 * phases :]
    chips, share, _ = ins[0].shape
    far, near = outs[: chips // 2], outs[chips // 2 :]
    for n, out in enumerate(far):
        for side in range(2):
            out[side * share : (side + 1) * share, :] = ins[2 * phases - 2 + side][chips // 2 + n]
        if phases == 1:
            put_face(face, out, 2 * share)
    for n, out in enumerate(near):
        for side in range(2 * phases):
            out[side * share : (side + 1) * share, :] = ins[side][1 + n]
        put_face(face, out, 2 * phases * share)


def assemble(face, parts):
    chips, share, cols = parts[0].shape
    phases = len(parts) // 2
    far = jax.ShapeDtypeStruct((2 * share + (8 if phases == 1 else 0), cols), jnp.bfloat16)
    near = jax.ShapeDtypeStruct((4 * share + 8, cols), jnp.bfloat16)
    shapes = [far] * (chips // 2) + ([near] * (chips // 2 - 1) if phases == 2 else [])
    return pl.pallas_call(
        functools.partial(assemble_kernel, phases),
        out_shape=shapes,
        in_specs=[VMEM] * (1 + len(parts)),
        out_specs=[VMEM] * len(shapes),
        cost_estimate=pl.CostEstimate(
            flops=0, bytes_accessed=4 * chips * share * cols * 2, transcendentals=0
        ),
        compiler_params=pltpu.CompilerParams(vmem_limit_bytes=4 * 2**20),
        name="assemble",
    )(face, *parts)


def coefficient_kernel(ks, first_row, scal, row_c, symbols, *refs):
    packs, outs = refs[: len(ks)], refs[-5:]
    first, second, cross, ahead, behind = outs
    core, chip = scal[0], scal[1]
    rc = 0.5 * row_c[...]
    inverse_rc = 1.0 / rc
    one, two, skew = symbols[0], symbols[1], symbols[2]
    for k, pack in zip(ks, packs):
        face = 0.5 * (pack[...] if k == 0 else get_face(pack, first_row))
        for j in range(4):
            side = core if j < 2 else 1 - core
            at = (chip ^ k) * 4 + side * 2 + j % 2
            cc = face[j : j + 1, :]
            cl = pltpu.roll(cc, 1, 1)
            diag = 2.0 * rc + cc + cl
            p0 = one + diag
            p1 = two + diag
            inverse = rc / (p0 * p1 + skew * skew)
            first[at] = p1 * inverse
            second[at] = p0 * inverse
            cross[at] = skew * inverse
            ahead[at] = cc * inverse_rc
            behind[at] = cl * inverse_rc


def coefficients(scal, row_c, symbols, ks, packs, first_row, before, chips):
    rows = 4 * chips
    pairs = symbols.shape[1]
    cols = row_c.shape[1]
    big = jax.ShapeDtypeStruct((rows, pairs, cols), jnp.float32)
    thin = jax.ShapeDtypeStruct((rows, 1, cols), jnp.float32)
    count = 3 + len(ks)
    return pl.pallas_call(
        functools.partial(coefficient_kernel, ks, first_row),
        out_shape=[big, big, big, thin, thin],
        in_specs=[SMEM] + [VMEM] * (2 + len(ks)) + [pl.BlockSpec(memory_space=pl.ANY)] * len(before),
        out_specs=[VMEM] * 5,
        input_output_aliases={count + n: n for n in range(len(before))},
        cost_estimate=pl.CostEstimate(
            flops=40 * len(ks) * pairs * cols,
            bytes_accessed=48 * len(ks) * pairs * cols,
            transcendentals=0,
        ),
        compiler_params=pltpu.CompilerParams(vmem_limit_bytes=8 * 2**20),
        name="coefficients",
    )(scal, row_c, symbols, *packs, *before)


def sweep_kernel(scal, row_c, first, second, cross, ahead, behind, *refs):
    *blocks, out, w_re, w_im, a_re, a_im, b_re, b_im, mixed = refs
    core, chip = scal[0], scal[1]
    rows, pairs, cols = w_re.shape
    chips = rows // 4
    share = 2 * pairs
    group = math.gcd(rows, 8)
    scale = 2.0 / row_c[...]

    def solve(i, t0, t1):
        s = cross[i]
        return first[i] * t0 + s * t1, second[i] * t1 - s * t0

    def enter(block, k, side, outer):
        owner = core if side == 0 else 1 - core
        row = owner if outer else 1 - owner
        i = (chip ^ k) * 4 + owner * 2 + row
        both = block.astype(jnp.float32)
        w_re[i], w_im[i] = solve(i, scale * both[:pairs], scale * both[pairs:])

    own_in, other_in, own_out, other_out = blocks[:4]
    far_in = blocks[4 : 4 + chips // 2]
    far_out = blocks[4 + chips // 2 : 4 + chips]
    near = blocks[4 + chips :]
    for side, block in enumerate((own_in, other_in, own_out, other_out)):
        enter(block[0], 0, side % 2, side >= 2)
    for outer, packs in ((False, far_in), (True, far_out)):
        for n, pack in enumerate(packs):
            for side in range(2):
                enter(pack[side * share : (side + 1) * share, :], chips // 2 + n, side, outer)
    for n, pack in enumerate(near):
        for side in range(4):
            enter(pack[side * share : (side + 1) * share, :], 1 + n, side % 2, side >= 2)

    def sweep(src, dst):
        def at(q, carry):
            i0 = q * group
            lines = [jnp.where(i0 == 0, rows - 1, i0 - 1)]
            lines += [i0 + n for n in range(group)]
            lines += [jnp.where(i0 + group == rows, 0, i0 + group)]
            for up, i, down in zip(lines, lines[1:], lines[2:]):
                u = []
                for z in src:
                    c = z[i]
                    u.append(
                        (z[up] + z[down])
                        + ahead[i] * pltpu.roll(c, cols - 1, 1)
                        + behind[i] * pltpu.roll(c, 1, 1)
                    )
                z0, z1 = solve(i, *u)
                z0, z1 = w_re[i] + z0, w_im[i] + z1
                if dst is not None:
                    dst[0][i], dst[1][i] = z0, z1
                    continue
                for j in range(mixed.shape[0]):
                    lanes = slice(j * 128, (j + 1) * 128)
                    mixed[j, pl.ds(0, pairs, stride=2), :] = z0[:, lanes]
                    mixed[j, pl.ds(1, pairs, stride=2), :] = z1[:, lanes]
                    out[i, :, lanes] = mixed[j].astype(out.dtype)
            return carry

        lax.fori_loop(0, rows // group, at, 0)

    src = (w_re, w_im)
    spaces = ((a_re, a_im), (b_re, b_im))
    for step in range(SWEEPS - 1):
        dst = None if step == SWEEPS - 2 else spaces[step % 2]
        sweep(src, dst)
        src = dst


def sweeps(scal, row_c, coeffs, blocks):
    rows, pairs, cols = coeffs[0].shape
    return pl.pallas_call(
        sweep_kernel,
        out_shape=jax.ShapeDtypeStruct((rows, 2 * pairs, cols), jnp.bfloat16),
        in_specs=[SMEM] + [VMEM] * (6 + len(blocks)),
        out_specs=VMEM,
        scratch_shapes=[pltpu.VMEM((rows, pairs, cols), jnp.float32)] * 6
        + [pltpu.VMEM((cols // 128, 2 * pairs, 128), jnp.float32)],
        cost_estimate=pl.CostEstimate(
            flops=80 * rows * pairs * cols, bytes_accessed=60 * rows * pairs * cols, transcendentals=0
        ),
        compiler_params=pltpu.CompilerParams(vmem_limit_bytes=16 * 2**20),
        name="sweeps",
    )(scal, row_c, *coeffs, *blocks)


def on_device(field, history, source, row_conduct, col_conduct):
    devices = lax.axis_size("space")
    chips = devices // 2
    steps, cols = field.shape[1:]
    share = steps // devices
    me = lax.axis_index("space")
    core, chip = me % 2, me // 2
    scal = jnp.stack([core, chip]).astype(jnp.int32)
    row_c = row_conduct.reshape(1, cols)
    partner = [(i, i ^ 1) for i in range(devices)]
    across = [(i, (i - 1 if i % 2 == 0 else i + 1) % devices) for i in range(devices)]
    tables = transform_tables(steps, devices)
    earlier = jnp.pad(
        jnp.transpose(history, (1, 0, 2)).astype(jnp.float32), ((0, 0), (5, 0), (0, 0))
    )
    args = (earlier, source, row_c, col_conduct, tables, devices)

    def send(x, pairs):
        return lax.ppermute(x, "space", pairs)

    def between(pack, k):
        return send(pack, [(i, i ^ (2 * k)) for i in range(devices)])

    halo = send(lax.dynamic_slice_in_dim(field, 1 - core, 1, 0), partner)
    face = jnp.concatenate([col_conduct, send(col_conduct, partner)], axis=0)
    own_in, other_in, spare = transform(False, scal, field, halo, *args)
    other_in = send(other_in, partner)
    halo = send(spare, across)
    packs = assemble(face, (own_in, other_in))
    far = range(chips // 2, chips)
    near = range(1, chips // 2)
    far_in = [between(pack, k) for pack, k in zip(packs, far)]
    own_out, other_out = transform(True, scal, field, halo, *args)
    other_out = send(other_out, partner)
    packs = assemble(face, (own_in, other_in, own_out, other_out))
    far_out = [between(pack, k) for pack, k in zip(packs, far)]
    near_all = [between(pack, k) for pack, k in zip(packs[chips // 2 :], near)]

    pairs = share // 2
    symbols = lax.dynamic_slice_in_dim(jnp.asarray(symbol_tables(steps)), me * pairs, pairs, 1)
    symbols = symbols[:, :, None]
    coeffs = coefficients(scal, row_c, symbols, (0, *far), (face, *far_in), 2 * share, (), chips)
    coeffs = coefficients(
        scal, row_c, symbols, tuple(near), near_all, 4 * share, coeffs, chips
    )
    blocks = (own_in, other_in, own_out, other_out, *far_in, *far_out, *near_all)
    return sweeps(scal, row_c, coeffs, blocks)


def solution(mesh):
    in_specs = (
        P(("groups", "space"), None, None),
        P(None, ("groups", "space"), None),
        P(("groups", "space"), None, None),
        P("groups"),
        P(("groups", "space"), None),
    )
    out_specs = P("groups", "space", None)

    return jax.shard_map(
        on_device, mesh=mesh, in_specs=in_specs, out_specs=out_specs, check_vma=False
    )
```

```python
import functools
import math

import jax
import jax.numpy as jnp
import numpy as np
from jax import lax
from jax.experimental import pallas as pl
from jax.experimental.pallas import tpu as pltpu
from jax.sharding import PartitionSpec as P

VMEM = pl.BlockSpec(memory_space=pltpu.VMEM)
SMEM = pl.BlockSpec(memory_space=pltpu.SMEM)
HBM = pl.BlockSpec(memory_space=pltpu.HBM)


def slot_order(steps, devices):
    share = steps // devices
    order = []
    for core in range(2):
        for chip in range(devices // 2):
            first = (chip * 2 + core) * share
            order += list(range(first, first + share, 2)) + list(range(first + 1, first + share, 2))
    return np.array(order)


def transform_tables(steps, devices):
    index = np.arange(steps)
    freqs = np.where(index == 1, steps // 2, index // 2)
    use_cos = (index % 2 == 0) | (index == 1)
    phase = 2.0 * np.pi / steps * (freqs[:, None] * index[None, :] % steps)
    table = np.where(use_cos[:, None], np.cos(phase), -np.sin(phase)) / math.sqrt(steps)
    table = table[slot_order(steps, devices)]
    high = table.astype(jnp.bfloat16)
    low = (table - high.astype(np.float64)).astype(jnp.bfloat16)
    return high, low


def symbol_tables(steps, devices):
    pair = np.arange(steps // 2)

    def real_part(freq):
        theta = 2.0 * np.pi / steps * freq
        return 11.0 / 6.0 - 3.0 * np.cos(theta) + 1.5 * np.cos(2.0 * theta) - np.cos(3.0 * theta) / 3.0

    theta = 2.0 * np.pi / steps * pair
    cross = 3.0 * np.sin(theta) - 1.5 * np.sin(2.0 * theta) + np.sin(3.0 * theta) / 3.0
    second = np.where(pair == 0, steps // 2, pair)
    table = np.stack([real_part(pair), real_part(second), cross]).astype(np.float32)
    table = table.reshape(3, devices, -1).transpose(1, 0, 2)
    return np.repeat(table[..., None], 128, axis=3)


def call(kernel, args, out, specs, mib, flops=0, scratch=(), aliases=None, out_specs=None):
    size = sum(math.prod(x.shape) * x.dtype.itemsize for x in (*args, *out))
    return pl.pallas_call(
        kernel,
        out_shape=list(out),
        in_specs=list(specs),
        out_specs=out_specs or [VMEM] * len(out),
        scratch_shapes=list(scratch),
        input_output_aliases=aliases or {},
        cost_estimate=pl.CostEstimate(flops=flops, bytes_accessed=size, transcendentals=0),
        compiler_params=pltpu.CompilerParams(vmem_limit_bytes=int(mib * 2**20)),
    )(*args)


def form_residual(outer, scal, centre, beside, hist, source, row_c, col_c, steps, put):
    row = scal[0] if outer else 1 - scal[0]
    cols = row_c.shape[1]
    rc = 0.5 * row_c[...]
    cc = 0.5 * col_c[pl.ds(row, 1)]
    cl = pltpu.roll(cc, 1, 1)
    diag = 11.0 / 6.0 + (2.0 * rc + cc + cl)
    tile = 16

    def at(i, before):
        rows = pl.ds(pl.multiple_of(i * tile, tile), tile)
        c = centre[0, rows, :].astype(jnp.float32)
        seq = jnp.concatenate([before, c], axis=0)
        r = source[row, rows, :].astype(jnp.float32) + 3.0 * seq[7 : 7 + tile]
        r -= 1.5 * seq[6 : 6 + tile]
        r += (1.0 / 3.0) * seq[5 : 5 + tile]
        near = beside[0, rows, :].astype(jnp.float32)
        r += rc * near
        r += cc * pltpu.roll(c, cols - 1, 1) + cl * pltpu.roll(c, 1, 1)
        put(rows, r - diag * c)
        return c[tile - 8 :]

    early = jnp.zeros((5, cols), jnp.float32)
    old = hist[...].astype(jnp.float32)
    old = [jnp.where(row == 0, old[n, 0:1], old[n, 1:2]) for n in range(3)]
    lax.fori_loop(0, steps // tile, at, jnp.concatenate([early, *old], axis=0))


def put_split(r_high, r_low):
    def put(rows, r):
        upper = r.astype(jnp.bfloat16)
        r_high[rows, :] = upper
        r_low[rows, :] = (r - upper.astype(jnp.float32)).astype(jnp.bfloat16)

    return put


def transform_rows(scal, high, low, own, other, r_high, r_low):
    core, chip = scal[0], scal[1]
    steps, cols = r_high.shape
    half = steps // 2
    chips, share, _ = own.shape
    width = min(cols, 256)
    for ref, which in ((other, 1 - core), (own, core)):
        part = pl.ds(pl.multiple_of(which * half, half), half)
        for j in range(0, cols, width):
            a, b = r_high[:, j : j + width], r_low[:, j : j + width]
            acc = jnp.dot(high[part, :], a, preferred_element_type=jnp.float32)
            acc += jnp.dot(high[part, :], b, preferred_element_type=jnp.float32)
            acc += jnp.dot(low[part, :], a, preferred_element_type=jnp.float32)
            acc = acc.astype(jnp.bfloat16)
            for g in range(chips):
                ref[g ^ chip, :, j : j + width] = acc[g * share : (g + 1) * share]


def local_kernel(outer, scal, centre, beside, hist, source, row_c, col_c, res):
    def put(rows, r):
        res[rows, :] = r

    steps = res.shape[0]
    form_residual(outer, scal, centre, beside, hist, source, row_c, col_c, steps, put)


def transform_kernel(scal, res, halo, row_c, high, low, own, other, r_high, r_low):
    steps = res.shape[0]
    tile = 64 if steps % 64 == 0 else 16
    rc = 0.5 * row_c[...]
    put = put_split(r_high, r_low)

    @pl.loop(0, steps // tile)
    def _(i):
        rows = pl.ds(pl.multiple_of(i * tile, tile), tile)
        put(rows, res[rows, :] + rc * halo[0, rows, :].astype(jnp.float32))

    transform_rows(scal, high, low, own, other, r_high, r_low)


def transform(args, devices):
    steps, cols = args[1].shape
    out = [jax.ShapeDtypeStruct((devices // 2, steps // devices, cols), jnp.bfloat16)] * 2
    scratch = [pltpu.VMEM((steps, cols), jnp.bfloat16)] * 2
    specs = [SMEM] + [VMEM] * (len(args) - 1)
    return call(transform_kernel, args, out, specs, 4, 6 * steps * steps * cols, scratch)


def form_local(outer, scal, centre, *fixed):
    _, steps, cols = centre.shape
    args = (scal, centre, *fixed)
    out = [jax.ShapeDtypeStruct((steps, cols), jnp.float32)]
    specs = [SMEM] + [VMEM] * 6
    kernel = functools.partial(local_kernel, outer)
    return call(kernel, args, out, specs, 4, 30 * steps * cols)[0]


def put_face(mine, theirs, out, first):
    face = jnp.concatenate([mine[...], theirs[...]], axis=0)
    high = face.astype(jnp.bfloat16)
    low = (face - high.astype(jnp.float32)).astype(jnp.bfloat16)
    out[first : first + 8, :] = jnp.concatenate([high, low], axis=0)


def get_face(pack, first):
    both = pack[first : first + 8, :].astype(jnp.float32)
    return both[:4] + both[4:]


def put_rows(out, first, *blocks):
    for block in blocks:
        out[first : first + block.shape[0], :] = block
        first += block.shape[0]


def pack_inner_kernel(own, other, mine, theirs, *outs):
    share = own.shape[1]
    for m, out in enumerate(outs, 1):
        put_rows(out, 0, own[2 * m], other[2 * m], own[2 * m + 1], other[2 * m + 1])
        put_face(mine, theirs, out, 4 * share)


def pack_outer_kernel(own, other, own_in, other_in, mine, theirs, *outs):
    *packs, cross, side = outs
    share = own.shape[1]
    middle = own.shape[0] // 4
    for m, out in enumerate(packs, 1):
        put_rows(out, 0, own[2 * m], other[2 * m], own[2 * m + 1], other[2 * m + 1])
    for m in range(middle):
        k = 2 * (middle + m) + 1
        put_rows(cross, m * 2 * share, own[k], other[k])
    put_rows(side, 0, own[1], other[1], own_in[1], other_in[1])
    put_face(mine, theirs, side, 4 * share)


def pack_far_kernel(own, other, cross, *outs):
    share = own.shape[1]
    middle = len(outs)
    for m, out in enumerate(outs):
        k = 2 * (middle + m)
        rows = cross[m * 2 * share : (m + 1) * 2 * share, :]
        put_rows(out, 0, own[k], other[k], rows)


def pack_near_kernel(*refs):
    *packs, out = refs
    count = len(packs) // 2
    rows = out.shape[0] // count
    for m, (inner, outer) in enumerate(zip(packs[:count], packs[count:])):
        first = outer.shape[0] // 2
        put_rows(out, m * rows, inner[first:, :], outer[first:, :])


def pack_rest_kernel(*refs):
    *packs, out = refs
    rows = out.shape[0] // len(packs)
    for m, ref in enumerate(packs):
        put_rows(out, m * rows, ref[ref.shape[0] - rows :, :])


def pack(kernel, args, *rows):
    cols = args[0].shape[-1]
    out = [jax.ShapeDtypeStruct((count, cols), jnp.bfloat16) for count in rows]
    return call(kernel, args, out, [VMEM] * len(args), 2)


def solve(first, second, cross, i, t0, t1):
    skew = cross[i]
    return first[i] * t0 + skew * t1, second[i] * t1 - skew * t0


def place(scal, k, side, outer):
    owner = scal[0] if side == 0 else 1 - scal[0]
    return (scal[1] ^ k) * 4 + owner * 2 + (owner if outer else 1 - owner)


def set_coefficients(scal, row_c, symbols, k, face, coeffs):
    first, second, cross, ahead, behind = coeffs
    cols = row_c.shape[1]
    rc = 0.5 * row_c[...]
    inverse_rc = 1.0 / rc
    me = scal[1] * 2 + scal[0]
    one, two, skew = (jnp.tile(symbols[me, n], (1, cols // 128)) for n in range(3))
    face = 0.5 * face
    for j in range(4):
        owner = scal[0] if j < 2 else 1 - scal[0]
        at = (scal[1] ^ k) * 4 + owner * 2 + j % 2
        cc = face[j : j + 1, :]
        cl = pltpu.roll(cc, 1, 1)
        diag = 2.0 * rc + cc + cl
        p0 = one + diag
        p1 = two + diag
        inverse = rc / (p0 * p1 + skew * skew)
        first[at] = p1 * inverse
        second[at] = p0 * inverse
        cross[at] = skew * inverse
        ahead[at] = cc * inverse_rc
        behind[at] = cl * inverse_rc


def enter(scal, row_c, k, outer, ref, first, coeffs, w):
    share = 2 * w[0].shape[1]
    scale = 2.0 / row_c[...]
    for side in range(2):
        i = place(scal, k, side, outer)
        at = first + side * share
        both = ref[at : at + share, :].astype(jnp.float32)
        t0, t1 = scale * both[: share // 2], scale * both[share // 2 :]
        w[0][i], w[1][i] = solve(*coeffs[:3], i, t0, t1)


def enter_pair(scal, row_c, k, outer, refs, coeffs, w):
    share = 2 * w[0].shape[1]
    scale = 2.0 / row_c[...]
    for side, ref in enumerate(refs):
        i = place(scal, k, side, outer)
        both = ref[k].astype(jnp.float32)
        t0, t1 = scale * both[: share // 2], scale * both[share // 2 :]
        w[0][i], w[1][i] = solve(*coeffs[:3], i, t0, t1)


def prepare_kernel(scal, row_c, symbols, mine, theirs, *refs):
    own_in, other_in, own_out, other_out, side, *packs = refs[:-7]
    coeffs, w = refs[-7:-2], refs[-2:]
    share = 2 * w[0].shape[1]
    shared = (scal, row_c)
    set_coefficients(*shared, symbols, 0, jnp.concatenate([mine[...], theirs[...]], axis=0), coeffs)
    enter_pair(*shared, 0, False, (own_in, other_in), coeffs, w)
    enter_pair(*shared, 0, True, (own_out, other_out), coeffs, w)
    set_coefficients(*shared, symbols, 1, get_face(side, 4 * share), coeffs)
    enter(*shared, 1, True, side, 0, coeffs, w)
    enter(*shared, 1, False, side, 2 * share, coeffs, w)
    for m, ref in enumerate(packs, 1):
        set_coefficients(*shared, symbols, 2 * m, get_face(ref, 4 * share), coeffs)
        enter(*shared, 2 * m, False, ref, 0, coeffs, w)


def complete_kernel(scal, row_c, symbols, rest, *refs):
    coeffs, w = refs[-7:-2], refs[-2:]
    share = 2 * w[0].shape[1]
    shared = (scal, row_c)
    far = w[0].shape[0] // 16
    for m in range(far):
        k = 2 * (far + m) + 1
        at = m * (2 * share + 8)
        set_coefficients(*shared, symbols, k, get_face(rest, at + 2 * share), coeffs)
        enter(*shared, k, False, rest, at, coeffs, w)


def relax_rows(start, count, coeffs, w, src, put):
    ahead, behind = coeffs[3:]
    rows, _, cols = w[0].shape
    group = max(d for d in range(1, 13) if count % d == 0)

    def wrap(i):
        return i & (rows - 1) if rows & (rows - 1) == 0 else lax.rem(i, rows)

    @pl.loop(0, count // group)
    def _(q):
        first = start + q * group
        lines = [wrap(first + rows - 1)] + [wrap(first + n) for n in range(group + 1)]
        for n, (up, i, down) in enumerate(zip(lines, lines[1:], lines[2:])):
            u = []
            for z in src:
                c = z[i]
                u.append(
                    (z[up] + z[down])
                    + ahead[i] * pltpu.roll(c, cols - 1, 1)
                    + behind[i] * pltpu.roll(c, 1, 1)
                )
            z0, z1 = solve(*coeffs[:3], i, *u)
            put(q * group + n, i, w[0][i] + z0, w[1][i] + z1)


def store_to(dst):
    def put(n, i, z0, z1):
        dst[0][i], dst[1][i] = z0, z1

    return put


def mix_to(out, mixed, after=None):
    pairs = mixed.shape[1] // 2

    def put(n, i, z0, z1):
        for j in range(mixed.shape[0]):
            lanes = slice(j * 128, (j + 1) * 128)
            mixed[j, pl.ds(0, pairs, stride=2), :] = z0[:, lanes]
            mixed[j, pl.ds(1, pairs, stride=2), :] = z1[:, lanes]
            out[n, :, lanes] = mixed[j].astype(out.dtype)
        if after is not None:
            after(n, i)

    return put


def halfway_kernel(scal, row_c, symbols, passed, *refs):
    packs, outs = refs[:-20], refs[-13:]
    coeffs, w, a, b, early, mixed = outs[:5], outs[5:7], outs[7:9], outs[9:11], outs[11], outs[12]
    share = 2 * w[0].shape[1]
    shared = (scal, row_c)
    for m, ref in enumerate(packs, 1):
        enter(*shared, 2 * m, True, ref, 0, coeffs, w)
        at = (m - 1) * (4 * share + 8)
        set_coefficients(*shared, symbols, 2 * m + 1, get_face(passed, at + 2 * share), coeffs)
        enter(*shared, 2 * m + 1, False, passed, at, coeffs, w)
        enter(*shared, 2 * m + 1, True, passed, at + 2 * share + 8, coeffs, w)
    half = w[0].shape[0] // 2
    base = (scal[1] * 4) // half * half
    relax_rows(base + 1, half - 2, coeffs, w, w, store_to(a))
    relax_rows(base + 2, half - 4, coeffs, w, a, store_to(b))
    relax_rows(base + 3, half - 6, coeffs, w, b, mix_to(early, mixed))


def finish_kernel(scal, row_c, *refs):
    coeffs, early, *rest = refs[:5], *refs[5:]
    *packs, out, w0, w1, a0, a1, b0, b1, done, mixed, sems = rest
    packs = packs[:-6]
    w, a, b = (w0, w1), (a0, a1), (b0, b1)
    rows, pairs, _ = w0.shape
    share = 2 * pairs
    half = rows // 2
    base = (scal[1] * 4) // half * half
    head = pltpu.make_async_copy(early, out.at[pl.ds(base + 3, half - 6)], sems.at[half + 6])
    head.start()
    for m, ref in enumerate(packs, len(packs)):
        enter(scal, row_c, 2 * m, True, ref, 0, coeffs, w)
        enter(scal, row_c, 2 * m + 1, True, ref, 2 * share, coeffs, w)

    def row_copy(n, i):
        return pltpu.make_async_copy(done.at[n], out.at[i], sems.at[n])

    relax_rows(base + half - 1, half + 2, coeffs, w, w, store_to(a))
    relax_rows(base + half - 2, half + 4, coeffs, w, a, store_to(b))
    put = mix_to(done, mixed, lambda n, i: row_copy(n, i).start())
    relax_rows(base + half - 3, half + 6, coeffs, w, b, put)
    head.wait()

    @pl.loop(0, half + 6)
    def _(n):
        row_copy(n, 0).wait()


def state_shapes(rows, pairs, cols):
    big = jax.ShapeDtypeStruct((rows, pairs, cols), jnp.float32)
    thin = jax.ShapeDtypeStruct((rows, 1, cols), jnp.float32)
    return [big, big, big, thin, thin] + [big] * 6


def prepare(scal, row_c, symbols, args, rows, pairs, state=()):
    kernel, _ = (complete_kernel, "complete") if state else (prepare_kernel, "prepare")
    cols = row_c.shape[1]
    args = (scal, row_c, symbols, *args, *state)
    out = state_shapes(rows, pairs, cols)[:7]
    specs = [SMEM] + [VMEM] * (len(args) - 1)
    first = len(args) - len(state)
    aliases = {first + n: n for n in range(len(state))}
    flops = 10 * rows * pairs * cols
    return call(kernel, args, out, specs, 4, flops, aliases=aliases)


def halfway(scal, row_c, symbols, passed, packs, state, rows, pairs):
    cols = row_c.shape[1]
    out = state_shapes(rows, pairs, cols)
    out += [jax.ShapeDtypeStruct((rows // 2 - 6, 2 * pairs, cols), jnp.bfloat16)]
    args = (scal, row_c, symbols, passed, *packs, *state)
    specs = [SMEM] + [VMEM] * (len(args) - 1)
    aliases = {4 + len(packs) + n: n for n in range(7)}
    scratch = [pltpu.VMEM((cols // 128, 2 * pairs, 128), jnp.float32)]
    flops = 40 * rows * pairs * cols
    return call(halfway_kernel, args, out, specs, 4, flops, scratch, aliases)


def finish(scal, row_c, state, packs):
    *state, early = state
    rows, pairs, cols = state[0].shape
    out = [jax.ShapeDtypeStruct((rows, 2 * pairs, cols), jnp.bfloat16)]
    out += [jax.ShapeDtypeStruct(x.shape, x.dtype) for x in state[5:]]
    args = (scal, row_c, *state[:5], early, *packs, *state[5:])
    specs = [SMEM] + [VMEM] * (len(args) - 1)
    aliases = {8 + len(packs) + n: 1 + n for n in range(6)}
    scratch = [
        pltpu.VMEM((rows // 2 + 6, 2 * pairs, cols), jnp.bfloat16),
        pltpu.VMEM((cols // 128, 2 * pairs, 128), jnp.float32),
        pltpu.SemaphoreType.DMA((rows // 2 + 7,)),
    ]
    flops = 50 * rows * pairs * cols
    out_specs = [HBM] + [VMEM] * 6
    return call(finish_kernel, args, out, specs, 8, flops, scratch, aliases, out_specs)[0]


def on_device(field, history, source, row_conduct, col_conduct):
    devices = lax.axis_size("space")
    lines = devices // 4
    steps, cols = field.shape[1:]
    share = steps // devices
    me = lax.axis_index("space")
    core, chip = me % 2, me // 2
    scal = jnp.stack([core, chip]).astype(jnp.int32)
    row_c = row_conduct.reshape(1, cols)
    across = [(i, (i - 1 if i % 2 == 0 else i + 1) % devices) for i in range(devices)]
    tables = transform_tables(steps, devices)
    symbols = symbol_tables(steps, devices)

    def send(x, pairs):
        if isinstance(pairs, int):
            pairs = [(i, i ^ pairs) for i in range(devices)]
        return lax.ppermute(x, "space", pairs)

    outside = lax.dynamic_slice_in_dim(field, core, 1, 0)
    field, outside = lax.optimization_barrier((field, outside))
    inside = lax.dynamic_slice_in_dim(field, 1 - core, 1, 0)
    halo_out = send(outside, across)
    halo_in = send(inside, 1)
    theirs = send(col_conduct, 1)
    faces = (col_conduct, theirs)
    fixed = (history, source, row_c, col_conduct)
    local = form_local(False, scal, inside, outside, *fixed)
    args = (scal, local, halo_in, row_c, *tables)
    own_in, other_in = transform(args, devices)
    other_in = send(other_in, 1)
    args = (own_in, other_in, *faces)
    packs = pack(pack_inner_kernel, args, *[4 * share + 8] * (lines - 1))
    inner = [send(x, 4 * m) for m, x in enumerate(packs, 1)]
    local = form_local(True, scal, outside, inside, *fixed)
    args = (scal, local, halo_out, row_c, *tables)
    own_out, other_out = transform(args, devices)
    other_out = send(other_out, 1)
    middle = lines // 2
    args = (own_out, other_out, own_in, other_in, *faces)
    sizes = [4 * share] * (middle - 1) + [lines * share, 4 * share + 8]
    *packs, cross, side = pack(pack_outer_kernel, args, *sizes)
    beside = [send(x, 4 * m) for m, x in enumerate(packs, 1)]
    cross = send(cross, 2)
    side = send(side, 2)
    args = (own_out, other_out, cross)
    packs = pack(pack_far_kernel, args, *[4 * share] * middle)
    far = [send(x, 4 * m) for m, x in enumerate(packs, middle)]
    args = (*inner[: middle - 1], *beside)
    rows = (middle - 1) * (4 * share + 8)
    passed = pack(pack_near_kernel, args, rows)[0]
    passed = send(passed, 2)
    rows = middle * (2 * share + 8)
    rest = pack(pack_rest_kernel, inner[middle - 1 :], rows)[0]
    rest = send(rest, 2)
    rows, pairs = 2 * devices, share // 2
    args = (*faces, own_in, other_in, own_out, other_out, side, *inner)
    state = prepare(scal, row_c, symbols, args, rows, pairs)
    state = halfway(scal, row_c, symbols, passed, beside, state, rows, pairs)
    *state, a0, a1, b0, b1, early = state
    state = prepare(scal, row_c, symbols, (rest,), rows, pairs, tuple(state))
    state = (*state, a0, a1, b0, b1, early)
    return finish(scal, row_c, state, far)


def solution(mesh):
    in_specs = (
        P(("groups", "space"), None, None),
        P(None, ("groups", "space"), None),
        P(("groups", "space"), None, None),
        P("groups"),
        P(("groups", "space"), None),
    )
    out_specs = P("groups", "space", None)

    return jax.shard_map(
        on_device, mesh=mesh, in_specs=in_specs, out_specs=out_specs, check_vma=False
    )
```
